32 devices in a mesh: groups: 2 (over x), seq: 16 (over z, y, core).
Axes of the slice: x: 2, y: 2, z: 4, core: 2. Of those that a mesh axis runs over, the one named last changes fastest.
Arguments:
- images: bfloat16 [4, 2048, 3072], P('groups', 'seq'), parts along dimension 0, may hold values from -6 to 6
- w_qkv: bfloat16 [3072, 1152], replicated, may hold values from -0.109375 to 0.109375
- b_qkv: float32 [1152], replicated, may hold values from -3 to 3
- q_gain: float32 [128], replicated, may hold values from 0.5 to 2.5
- k_gain: float32 [128], replicated, may hold values from 0.5 to 2.5
- key_basis: float32 [3, 128, 32], replicated, may hold values from -0.5 to 0.5
- value_basis: float32 [3, 128, 32], replicated, may hold values from -0.5 to 0.5
- centers: float32 [4, 2, 3, 128], P('groups'), parts along dimension 0, may hold values from -22 to 22
- refresh: int32 [2, 3], replicated, may hold values 0 or 1
- w_out: bfloat16 [384, 3072], replicated, may hold values from -0.3125 to 0.3125
Outputs:
- mixed: bfloat16 [4, 2048, 3072], P('groups', 'seq'), parts along dimension 0
- new_centers: float32 [4, 2, 3, 128], P('groups'), parts along dimension 0
The draws below stay inside these ranges and needn't reach their ends.
There are 2 independent parts, one for each index of `groups`. The reference program is written for one: setup_inputs(seed, part) draws one part's arguments, and reference() takes and returns one part's arrays. A program takes and returns all parts, laid end to end along the dimension named above; an argument that names none is the same for every part. Nothing has to cross between parts.
All inputs are finite; a program needn't handle non-finite values.
Results may differ from the reference program's by a relative error of at most 0.0051.
Values may be sent and summed in bfloat16 or wider, within the bound.
A program may use at most 64 MiB of HBM per device.

```python
import math
import jax
import jax.numpy as jnp
from jax import lax

WIDTH = 3072
HEAD_DIM = 128
HEADS_DEV = 3
CODE_RANK = 32
SAMPLES = 2
TOK_DEV = 128
LENGTH = 2048
N_SEQ = 16


def draw_b_qkv(key, part):
    total = 3 * HEADS_DEV * HEAD_DIM
    drawn = 0.5 * jax.random.truncated_normal(jax.random.fold_in(key, 11), -6.0, 6.0, (total,), jnp.float32)
    return drawn


def draw_centers(key, part):
    shape = (SAMPLES, 2, HEADS_DEV, HEAD_DIM)
    return 0.5 * jax.random.truncated_normal(jax.random.fold_in(key, 24), -6.0, 6.0, shape, jnp.float32)


def with_ends(result, key, low, high):
    place = [jax.random.randint(jax.random.fold_in(key, axis), (), 0, length) for axis, length in enumerate(result.shape)]
    main_axis = result.shape.index(max(result.shape))
    next_to = place[:main_axis] + [(place[main_axis] + 1) % result.shape[main_axis]] + place[main_axis + 1:]
    return result.at[tuple(place)].set(low).at[tuple(next_to)].set(high)


def shard_levels(own_key, dims, cuts, low, top_value):
    def one(axis_at, parts):
        steps = jax.random.uniform(jax.random.fold_in(jax.random.fold_in(own_key, 6), axis_at), (parts,), jnp.float32, low / len(cuts), top_value / len(cuts))
        return jnp.repeat(jnp.exp(steps), dims[axis_at] // parts).reshape((-1,) + (1,) * (len(dims) - axis_at - 1))

    level = one(*cuts[0])
    for cut in cuts[1:]:
        level = level * one(*cut)
    return level


def noise(key, dims, spread, most, split=(), kind=jnp.bfloat16):
    array = jax.random.normal(key, dims, jnp.float32) * spread
    if len(split) > 0:
        array = shard_levels(key, dims, split, -0.22, 0.18) * array
    return jnp.clip(array, min=-most, max=most).astype(kind)


def setup_inputs(seed: int = 0, part: int = 0) -> dict:
    splits = jax.random.split(jax.random.key(seed), 11)
    part_keys = jax.random.split(jax.random.fold_in(splits[10], part), 11)
    images = noise(part_keys[0], (SAMPLES, LENGTH, WIDTH), 1.0, 6.0, ((1, 16),))
    w_qkv = noise(splits[1], (WIDTH, 3 * HEADS_DEV * HEAD_DIM), WIDTH ** -0.5, 0.109375)
    b_qkv = draw_b_qkv(jax.random.fold_in(splits[10], 71), part)
    q_gain = jnp.clip(jnp.exp(jax.random.uniform(splits[3], (HEAD_DIM,), jnp.float32, math.log(0.5), math.log(2.5))), 0.5, 2.5)
    k_gain = jnp.clip(jnp.exp(jax.random.uniform(splits[4], (HEAD_DIM,), jnp.float32, math.log(0.5), math.log(2.5))), 0.5, 2.5)
    key_basis = noise(splits[5], (HEADS_DEV, HEAD_DIM, CODE_RANK), HEAD_DIM ** -0.5, 0.5, (), jnp.float32)
    value_basis = noise(splits[6], (HEADS_DEV, HEAD_DIM, CODE_RANK), HEAD_DIM ** -0.5, 0.5, (), jnp.float32)
    centers = draw_centers(jax.random.fold_in(jax.random.fold_in(splits[10], part), 71), part)
    refresh = with_ends((jax.random.randint(splits[8], (2, HEADS_DEV), 0, 2) < 1).astype(jnp.int32), jax.random.fold_in(splits[8], 1), 0, 1)
    w_out = noise(splits[9], (HEADS_DEV * HEAD_DIM, WIDTH), (HEADS_DEV * HEAD_DIM) ** -0.5, 0.3125)
    return {"images": images, "w_qkv": w_qkv, "b_qkv": b_qkv, "q_gain": q_gain, "k_gain": k_gain, "key_basis": key_basis, "value_basis": value_basis, "centers": centers, "refresh": refresh, "w_out": w_out}


epsilon = 1e-06
highest = lax.Precision.HIGHEST

def normalize(values, gain):
    mean_square = lax.optimization_barrier(jnp.mean(values * values, axis=-1, keepdims=True))
    return values * lax.rsqrt(mean_square + epsilon) * gain

def reference(images, w_qkv, b_qkv, q_gain, k_gain, key_basis, value_basis, centers, refresh, w_out):
    sample_count, length, model_width = images.shape
    head_count, head_dim, code_rank = key_basis.shape
    factor = 1.0 / math.sqrt(head_dim)
    flat_images = images.reshape(sample_count * length, model_width)
    projected = jnp.dot(flat_images, w_qkv, preferred_element_type=jnp.float32) + b_qkv
    projected = projected.reshape(sample_count, length, 3, head_count, head_dim)
    query = normalize(projected[:, :, 0], q_gain)
    keys = normalize(projected[:, :, 1], k_gain)
    values = projected[:, :, 2]
    key_center = centers[:, 0]
    value_center = centers[:, 1]
    key_codes = jnp.einsum('blhd,hdr->blhr', keys - key_center[:, None], key_basis, precision=highest).astype(jnp.bfloat16)
    value_codes = jnp.einsum('blhd,hdr->blhr', values - value_center[:, None], value_basis, precision=highest).astype(jnp.bfloat16)
    key_rebuilt = jnp.einsum('blhr,hdr->blhd', key_codes.astype(jnp.float32), key_basis, precision=highest) + key_center[:, None]
    value_rebuilt = jnp.einsum('blhr,hdr->blhd', value_codes.astype(jnp.float32), value_basis, precision=highest) + value_center[:, None]
    fresh_means = jnp.stack([lax.optimization_barrier(jnp.mean(keys, axis=1)), lax.optimization_barrier(jnp.mean(values, axis=1))], axis=1)
    new_centers = jnp.where(refresh[None, :, :, None] == 1, fresh_means, centers)
    columns = jnp.arange(length, dtype=jnp.int32)

    def attend_block(block_index):
        first_row = (block_index * TOK_DEV).astype(jnp.int32)
        query_block = lax.dynamic_slice_in_dim(query, first_row, TOK_DEV, 1)
        key_block = lax.dynamic_slice_in_dim(keys, first_row, TOK_DEV, 1)
        value_block = lax.dynamic_slice_in_dim(values, first_row, TOK_DEV, 1)
        far_scores = jnp.einsum('bqhd,bshd->bhqs', query_block, key_rebuilt, precision=highest) * factor
        owned = (columns >= first_row) & (columns < first_row + TOK_DEV)
        far_scores = jnp.where(owned[None, None, None, :], -jnp.inf, far_scores)
        near_scores = jnp.einsum('bqhd,bshd->bhqs', query_block, key_block, precision=highest) * factor
        row_max = jnp.maximum(lax.optimization_barrier(jnp.max(far_scores, axis=-1)), lax.optimization_barrier(jnp.max(near_scores, axis=-1)))
        far_weights = jnp.exp(far_scores - row_max[..., None])
        near_weights = jnp.exp(near_scores - row_max[..., None])
        row_sum = lax.optimization_barrier(jnp.sum(far_weights, axis=-1)) + lax.optimization_barrier(jnp.sum(near_weights, axis=-1))
        weighted = jnp.einsum('bhqs,bshd->bhqd', far_weights, value_rebuilt, precision=highest)
        weighted = weighted + jnp.einsum('bhqs,bshd->bhqd', near_weights, value_block, precision=highest)
        return weighted / row_sum[..., None]
    blocks = lax.map(attend_block, jnp.arange(N_SEQ, dtype=jnp.int32))
    attended = blocks.transpose(1, 0, 3, 2, 4).reshape(sample_count * length, head_count * head_dim).astype(jnp.bfloat16)
    mixed = jnp.dot(attended, w_out, preferred_element_type=jnp.float32).astype(jnp.bfloat16)
    return (mixed.reshape(sample_count, length, model_width), new_centers)
```

```python
import functools
import math

import jax
import jax.numpy as jnp
from jax import lax
from jax.experimental import pallas as pl
from jax.experimental.pallas import tpu as pltpu
from jax.sharding import PartitionSpec as P

epsilon = 1e-06
highest = lax.Precision.HIGHEST
LANES = 128
ROW_CHUNKS = 6
MESH = pl.DeviceIdType.MESH
NT = (((1,), (1,)), ((), ()))


def natural_ring(mesh):
    try:
        names = list(mesh.axis_names)
        line = mesh.devices
        if names.index("seq") == 0:
            line = line.T
        chips = [d.coords for d in line[0][::2]]
        return all(
            sum(abs(a - b) for a, b in zip(one, two)) == 1 for one, two in zip(chips, chips[1:])
        )
    except Exception:
        return False


def attend_kernel(
    seq_count, natural,
    images, w_qkv, b_qkv, q_gain, k_gain, key_basis, value_basis, centers,
    attended, sums,
    x_s, w_s, b_s, qg_s, kg_s, kb_s, vb_s, cen_s,
    kv_acc, q_acc, kbd, vbd, kc_s, vc_s, qs_s, qbd,
    m_s, mn_s, ln_s, accn_s, acc_s,
    own, left_in, right_in, sib_own, sib_left, sib_right, part, part_in,
    in_sem, img_sem, small_sem,
    right_send, right_recv, left_send, left_recv,
    so_send, so_recv, sl_send, sl_recv, sr_send, sr_recv, p_send, p_recv,
):
    samples, tokens, width = x_s.shape
    heads, head_dim, rank = kb_s.shape
    codes = heads * rank
    side = heads * head_dim
    rows = samples * tokens
    chips = seq_count // 2
    half = chips // 2
    levels = seq_count.bit_length() - 1
    me = lax.axis_index("seq")
    core = me % 2
    chip = me // 2

    if natural:
        right_chip = (chip + 1) % chips
        left_chip = (chip + chips - 1) % chips
    else:
        def chip_at(pos):
            back = pos // half
            z = (1 - back) * pos + back * (chips - 1 - pos)
            return 2 * z + back

        far = chip % 2
        pos = (1 - far) * (chip // 2) + far * (chips - 1 - chip // 2)
        right_chip = chip_at((pos + 1) % chips)
        left_chip = chip_at((pos + chips - 1) % chips)
    right = right_chip * 2 + core
    left = left_chip * 2 + core
    sibling = chip * 2 + 1 - core
    partners = [me + bit * (1 - 2 * ((me // bit) % 2)) for bit in [1 << k for k in range(levels)]]

    barrier = pltpu.get_barrier_semaphore()
    greeted = [right, left] + partners
    for device in greeted:
        pl.semaphore_signal(barrier, inc=1, device_id={"seq": device}, device_id_type=MESH)

    step = width // ROW_CHUNKS
    img_copies, kv_copies = [], []
    for i in range(ROW_CHUNKS):
        cut = pl.ds(i * step, step)
        c = pltpu.make_async_copy(images.at[:, :, cut], x_s.at[:, :, cut], img_sem.at[i])
        c.start()
        img_copies.append(c)
        c = pltpu.make_async_copy(
            w_qkv.at[cut, pl.ds(side, 2 * side)], w_s.at[cut, pl.ds(side, 2 * side)], in_sem.at[i]
        )
        c.start()
        kv_copies.append(c)
    small = []
    pairs = [(b_qkv, b_s), (q_gain, qg_s), (k_gain, kg_s), (key_basis, kb_s), (value_basis, vb_s), (centers, cen_s)]
    for i, (src, dst) in enumerate(pairs):
        c = pltpu.make_async_copy(src, dst, small_sem.at[i])
        c.start()
        small.append(c)
    q_copy = pltpu.make_async_copy(
        w_qkv.at[:, pl.ds(0, side)], w_s.at[:, pl.ds(0, side)], in_sem.at[ROW_CHUNKS]
    )
    q_copy.start()

    for c in small:
        c.wait()
    kbd[...] = jnp.zeros_like(kbd)
    vbd[...] = jnp.zeros_like(vbd)
    for h in range(heads):
        kbd[h * head_dim:(h + 1) * head_dim, h * rank:(h + 1) * rank] = kb_s[h]
        vbd[h * head_dim:(h + 1) * head_dim, h * rank:(h + 1) * rank] = vb_s[h]

    for i in range(ROW_CHUNKS):
        img_copies[i].wait()
        kv_copies[i].wait()
        piece = jnp.dot(
            x_s[:, :, i * step:(i + 1) * step].reshape(rows, step),
            w_s[i * step:(i + 1) * step, side:3 * side],
            preferred_element_type=jnp.float32,
        )
        if i == 0:
            kv_acc[...] = piece
        else:
            kv_acc[...] += piece

    def gain_row(ref):
        return ref[...].reshape(1, head_dim)

    def bias_row(column):
        return b_s[pl.ds(column, head_dim)].reshape(1, head_dim)

    part[0] = jnp.zeros_like(part[0])
    for h in range(heads):
        cut = slice(h * head_dim, (h + 1) * head_dim)
        raw = kv_acc[:, cut] + bias_row(side + h * head_dim)
        mean_square = jnp.mean(raw * raw, axis=-1, keepdims=True)
        keys = raw * lax.rsqrt(mean_square + epsilon) * gain_row(kg_s)
        vcut = slice(side + h * head_dim, side + (h + 1) * head_dim)
        values = kv_acc[:, vcut] + bias_row(2 * side + h * head_dim)
        for b in range(samples):
            own_rows = slice(b * tokens, (b + 1) * tokens)
            for j, one in enumerate((keys, values)):
                line = (b * 2 + j) * heads + h
                part[0, line:line + 1, :] = jnp.sum(one[own_rows], axis=0, keepdims=True)
            kc_s[own_rows, cut] = keys[own_rows] - cen_s[b, 0, h:h + 1, :]
            vc_s[own_rows, cut] = values[own_rows] - cen_s[b, 1, h:h + 1, :]

    pl.semaphore_wait(barrier, len(greeted))
    started = []

    def send(src, dst, send_sem, recv_sem, device):
        c = pltpu.make_async_remote_copy(
            src_ref=src, dst_ref=dst, send_sem=send_sem, recv_sem=recv_sem,
            device_id={"seq": device}, device_id_type=MESH,
        )
        c.start()
        started.append(c)
        return c

    def goes(direction, distance, b):
        if distance < half or chips % 2:
            return True
        return (b < samples // 2) == (direction == 0)

    rights, lefts, sib_owns, sib_lefts, sib_rights = {}, {}, {}, {}, {}

    def send_right(distance, b):
        if distance <= half and goes(0, distance, b):
            src = own.at[b] if distance == 1 else left_in.at[distance - 2, b]
            rights[distance, b] = send(
                src, left_in.at[distance - 1, b], right_send.at[distance - 1, b],
                right_recv.at[distance - 1, b], right,
            )

    def send_left(distance, b):
        if distance <= half and goes(1, distance, b):
            src = own.at[b] if distance == 1 else right_in.at[distance - 2, b]
            lefts[distance, b] = send(
                src, right_in.at[distance - 1, b], left_send.at[distance - 1, b],
                left_recv.at[distance - 1, b], left,
            )

    for b in range(samples):
        own_rows = slice(b * tokens, (b + 1) * tokens)
        for j, (src, basis) in enumerate(((kc_s, kbd), (vc_s, vbd))):
            coded = jnp.dot(src[own_rows, :], basis[...], precision=highest, preferred_element_type=jnp.float32)
            own[b, j * codes:(j + 1) * codes, :] = coded.T[:codes].astype(jnp.bfloat16)
        send_right(1, b)
        send_left(1, b)
        sib_owns[b] = send(own.at[b], sib_own.at[b], so_send.at[b], so_recv.at[b], sibling)

    exchanges = []

    def exchange(level):
        if level > 0:
            exchanges[level - 1].wait_recv()
            part[level] = part[level - 1] + part_in[level - 1]
        if level < levels:
            exchanges.append(
                send(part.at[level], part_in.at[level], p_send.at[level], p_recv.at[level], partners[level])
            )

    exchange(0)

    q_copy.wait()
    q_acc[...] = jnp.dot(
        x_s[...].reshape(rows, width), w_s[:, :side], preferred_element_type=jnp.float32
    )
    scale = math.log2(math.e) / math.sqrt(head_dim)
    for h in range(heads):
        cut = slice(h * head_dim, (h + 1) * head_dim)
        raw = q_acc[:, cut] + bias_row(h * head_dim)
        mean_square = jnp.mean(raw * raw, axis=-1, keepdims=True)
        query = raw * lax.rsqrt(mean_square + epsilon) * gain_row(qg_s) * scale
        qs_s[:, cut] = query
        coded = jnp.dot(query, kbd[cut, :], precision=highest, preferred_element_type=jnp.float32)
        high = coded.astype(jnp.bfloat16)
        low = (coded - high.astype(jnp.float32)).astype(jnp.bfloat16)
        for b in range(samples):
            own_rows = slice(b * tokens, (b + 1) * tokens)
            qbd[b, h * tokens:(h + 1) * tokens, :LANES] = high[own_rows]
            qbd[b, h * tokens:(h + 1) * tokens, LANES:] = low[own_rows]

    def near(b):
        own_rows = slice(b * tokens, (b + 1) * tokens)
        for h in range(heads):
            cut = slice(h * head_dim, (h + 1) * head_dim)
            lines = slice(h * tokens, (h + 1) * tokens)
            scores = lax.dot_general(
                qs_s[own_rows, cut], kc_s[own_rows, cut], NT, precision=highest,
                preferred_element_type=jnp.float32,
            )
            top = jnp.max(scores, axis=-1, keepdims=True)
            weights = jnp.exp2(scores - top)
            total = jnp.sum(weights, axis=-1, keepdims=True)
            wide = jnp.broadcast_to(top, (tokens, LANES))
            m_s[b, lines, :] = wide
            mn_s[b, lines, :] = wide
            ln_s[b, lines, :] = jnp.broadcast_to(total, (tokens, LANES))
            accn_s[b, lines, :] = jnp.dot(
                weights, vc_s[own_rows, cut], precision=highest, preferred_element_type=jnp.float32
            )
        acc_s[b] = jnp.zeros_like(acc_s[b])

    def absorb(b, blocks):
        key_side = jnp.concatenate([r[:LANES, :] for r in blocks], axis=1)
        scores = jnp.dot(
            qbd[b], jnp.concatenate([key_side, key_side], axis=0), preferred_element_type=jnp.float32
        )
        before = m_s[b]
        now = jnp.maximum(before, jnp.max(scores, axis=-1, keepdims=True))
        weights = jnp.exp2(scores - now[:, :1]).astype(jnp.bfloat16)
        value_side = jnp.concatenate([r[codes:2 * codes, :] for r in blocks], axis=1)
        ones = jnp.ones((LANES - codes, value_side.shape[1]), jnp.bfloat16)
        added = lax.dot_general(
            weights, jnp.concatenate([value_side, ones], axis=0), NT, preferred_element_type=jnp.float32
        )
        acc_s[b] = acc_s[b] * jnp.exp2(before - now) + added
        m_s[b] = now

    for b in range(samples):
        near(b)

    waiting = {b: [] for b in range(samples)}
    for distance in range(1, half + 1):
        for b in range(samples):
            blocks = []
            if (distance, b) in rights:
                rights[distance, b].wait_recv()
                send_right(distance + 1, b)
                src = left_in.at[distance - 1, b]
                sib_lefts[distance, b] = send(
                    src, sib_left.at[distance - 1, b], sl_send.at[distance - 1, b],
                    sl_recv.at[distance - 1, b], sibling,
                )
                blocks.append(src)
            if (distance, b) in lefts:
                lefts[distance, b].wait_recv()
                send_left(distance + 1, b)
                src = right_in.at[distance - 1, b]
                sib_rights[distance, b] = send(
                    src, sib_right.at[distance - 1, b], sr_send.at[distance - 1, b],
                    sr_recv.at[distance - 1, b], sibling,
                )
                blocks.append(src)
            if distance == 1:
                sib_owns[b].wait_recv()
                blocks.append(sib_own.at[b])
            else:
                for copies, held in ((sib_lefts, sib_left), (sib_rights, sib_right)):
                    if (distance - 1, b) in copies:
                        copies[distance - 1, b].wait_recv()
                        blocks.append(held.at[distance - 2, b])
            absorb(b, blocks)
        if distance <= levels:
            exchange(distance)
    for level in range(half + 1, levels + 1):
        exchange(level)
    sums[...] = part[levels]

    for b in range(samples):
        own_rows = slice(b * tokens, (b + 1) * tokens)
        blocks = []
        for copies, held in ((sib_lefts, sib_left), (sib_rights, sib_right)):
            if (half, b) in copies:
                copies[half, b].wait_recv()
                blocks.append(held.at[half - 1, b])
        absorb(b, blocks)
        for h in range(heads):
            cut = slice(h * head_dim, (h + 1) * head_dim)
            lines = slice(h * tokens, (h + 1) * tokens)
            gathered = acc_s[b, lines, :]
            fade = jnp.exp2(mn_s[b, lines, :] - m_s[b, lines, :])
            total = gathered[:, codes:codes + 1] + (fade * ln_s[b, lines, :])[:, :1]
            rebuilt = lax.dot_general(
                gathered, vbd[cut, :], NT, precision=highest, preferred_element_type=jnp.float32
            )
            result = (rebuilt + fade * accn_s[b, lines, :]) / total + cen_s[b, 1, h:h + 1, :]
            attended[own_rows, cut] = result.astype(jnp.bfloat16)
    for c in started:
        c.wait_send()


def finish_kernel(length, refresh, attended, w_out, sums, centers, mixed, new_centers):
    samples, pair, heads, head_dim = new_centers.shape
    tokens = attended.shape[0] // samples
    product = jnp.dot(attended[...], w_out[...], preferred_element_type=jnp.float32)
    mixed[...] = product.astype(jnp.bfloat16).reshape(mixed.shape)

    @pl.when(pl.program_id(0) == 0)
    def _():
        for b in range(samples):
            for j in range(pair):
                for h in range(heads):
                    line = (b * pair + j) * heads + h
                    fresh = sums[line:line + 1, :] / length
                    old = centers[b, j, h:h + 1, :]
                    new_centers[b, j, h:h + 1, :] = jnp.where(refresh[j, h] == 1, fresh, old)


def per_device(
    seq_count, natural,
    images, w_qkv, b_qkv, q_gain, k_gain, key_basis, value_basis, centers, refresh, w_out
):
    samples, tokens, width = images.shape
    heads, head_dim, rank = key_basis.shape
    side = heads * head_dim
    rows = samples * tokens
    codes = heads * rank
    chips = seq_count // 2
    half = chips // 2
    levels = seq_count.bit_length() - 1
    lines = -(-samples * 2 * heads // 8) * 8
    f32, bf16 = jnp.float32, jnp.bfloat16
    any_spec = pl.BlockSpec(memory_space=pl.ANY)
    vmem_spec = pl.BlockSpec(memory_space=pltpu.VMEM)
    dma = pltpu.SemaphoreType.DMA
    block = (samples, 2 * codes, tokens)
    stat = pltpu.VMEM((samples, heads * tokens, LANES), f32)
    attended, sums = pl.pallas_call(
        functools.partial(attend_kernel, seq_count, natural),
        out_shape=(
            jax.ShapeDtypeStruct((rows, side), bf16),
            jax.ShapeDtypeStruct((lines, head_dim), f32),
        ),
        in_specs=[any_spec] * 8,
        out_specs=(vmem_spec, vmem_spec),
        scratch_shapes=[
            pltpu.VMEM(images.shape, bf16),
            pltpu.VMEM(w_qkv.shape, bf16),
            pltpu.VMEM(b_qkv.shape, f32),
            pltpu.VMEM(q_gain.shape, f32),
            pltpu.VMEM(k_gain.shape, f32),
            pltpu.VMEM(key_basis.shape, f32),
            pltpu.VMEM(value_basis.shape, f32),
            pltpu.VMEM(centers.shape, f32),
            pltpu.VMEM((rows, 2 * side), f32),
            pltpu.VMEM((rows, side), f32),
            pltpu.VMEM((side, LANES), f32),
            pltpu.VMEM((side, LANES), f32),
            pltpu.VMEM((rows, side), f32),
            pltpu.VMEM((rows, side), f32),
            pltpu.VMEM((rows, side), f32),
            pltpu.VMEM((samples, heads * tokens, 2 * LANES), bf16),
            stat, stat, stat, stat, stat,
            pltpu.VMEM(block, bf16),
            pltpu.VMEM((half,) + block, bf16),
            pltpu.VMEM((half,) + block, bf16),
            pltpu.VMEM(block, bf16),
            pltpu.VMEM((half,) + block, bf16),
            pltpu.VMEM((half,) + block, bf16),
            pltpu.VMEM((levels + 1, lines, head_dim), f32),
            pltpu.VMEM((levels, lines, head_dim), f32),
            dma((ROW_CHUNKS + 1,)), dma((ROW_CHUNKS,)), dma((6,)),
            dma((half, samples)), dma((half, samples)), dma((half, samples)), dma((half, samples)),
            dma((samples,)), dma((samples,)),
            dma((half, samples)), dma((half, samples)), dma((half, samples)), dma((half, samples)),
            dma((levels,)), dma((levels,)),
        ],
        compiler_params=pltpu.CompilerParams(
            collective_id=0, has_side_effects=True, vmem_limit_bytes=40 << 20
        ),
        name="attend",
    )(images, w_qkv, b_qkv, q_gain, k_gain, key_basis, value_basis, centers)

    tile = width // 3
    mixed, new_centers = pl.pallas_call(
        functools.partial(finish_kernel, float(tokens * seq_count)),
        grid=(width // tile,),
        out_shape=(
            jax.ShapeDtypeStruct(images.shape, bf16),
            jax.ShapeDtypeStruct(centers.shape, f32),
        ),
        in_specs=[
            pl.BlockSpec(memory_space=pltpu.SMEM),
            pl.BlockSpec((rows, side), lambda n: (0, 0)),
            pl.BlockSpec((side, tile), lambda n: (0, n)),
            pl.BlockSpec((lines, head_dim), lambda n: (0, 0)),
            pl.BlockSpec(centers.shape, lambda n: (0, 0, 0, 0)),
        ],
        out_specs=(
            pl.BlockSpec((samples, tokens, tile), lambda n: (0, 0, n)),
            pl.BlockSpec(centers.shape, lambda n: (0, 0, 0, 0)),
        ),
        compiler_params=pltpu.CompilerParams(vmem_limit_bytes=16 << 20),
        name="finish",
    )(refresh, attended, w_out, sums, centers)
    return mixed, new_centers


def solution(mesh):
    return jax.shard_map(
        functools.partial(per_device, mesh.shape["seq"], natural_ring(mesh)),
        mesh=mesh,
        in_specs=(
            P("groups", "seq", None),
            P(),
            P(),
            P(),
            P(),
            P(),
            P(),
            P("groups", None, None, None),
            P(),
            P(),
        ),
        out_specs=(P("groups", "seq", None), P("groups", None, None, None)),
        check_vma=False,
    )
```

```python
import functools
import math

import jax
import jax.numpy as jnp
from jax import lax
from jax.experimental import pallas as pl
from jax.experimental.pallas import tpu as pltpu
from jax.sharding import PartitionSpec as P

epsilon = 1e-06
highest = lax.Precision.HIGHEST
LANES = 128
ROW_CHUNKS = 6
OUT_TILES = 6
MESH = pl.DeviceIdType.MESH
NT = (((1,), (1,)), ((), ()))


def natural_ring(mesh):
    try:
        names = list(mesh.axis_names)
        line = mesh.devices
        if names.index("seq") == 0:
            line = line.T
        chips = [d.coords for d in line[0][::2]]
        return all(
            sum(abs(a - b) for a, b in zip(one, two)) == 1 for one, two in zip(chips, chips[1:])
        )
    except Exception:
        return False


def attend_kernel(
    seq_count, natural,
    images, w_qkv, b_qkv, q_gain, k_gain, key_basis, value_basis, centers,
    attended, sums,
    x_s, w_s, b_s, qg_s, kg_s, kb_s, vb_s, cen_s,
    kv_acc, q_acc, kbd, vbd, kc_s, vc_s, qs_s, qbd,
    m_s, mn_s, ln_s, accn_s, acc_s,
    own, left_in, right_in, sib_own, sib_left, sib_right, part, part_in,
    in_sem, img_sem, small_sem,
    right_send, right_recv, left_send, left_recv,
    so_send, so_recv, sl_send, sl_recv, sr_send, sr_recv, p_send, p_recv,
):
    samples, tokens, width = x_s.shape
    heads, rank, head_dim = kb_s.shape
    codes = heads * rank
    side = heads * head_dim
    rows = samples * tokens
    chips = seq_count // 2
    half = chips // 2
    levels = seq_count.bit_length() - 1
    me = lax.axis_index("seq")
    core = me % 2
    chip = me // 2

    if natural:
        right_chip = (chip + 1) % chips
        left_chip = (chip + chips - 1) % chips
    else:
        def chip_at(pos):
            back = pos // half
            z = (1 - back) * pos + back * (chips - 1 - pos)
            return 2 * z + back

        far = chip % 2
        pos = (1 - far) * (chip // 2) + far * (chips - 1 - chip // 2)
        right_chip = chip_at((pos + 1) % chips)
        left_chip = chip_at((pos + chips - 1) % chips)
    right = right_chip * 2 + core
    left = left_chip * 2 + core
    sibling = chip * 2 + 1 - core
    partners = [me + bit * (1 - 2 * ((me // bit) % 2)) for bit in [1 << k for k in range(levels)]]

    barrier = pltpu.get_barrier_semaphore()
    greeted = [right, left] + partners
    for device in greeted:
        pl.semaphore_signal(barrier, inc=1, device_id={"seq": device}, device_id_type=MESH)

    step = width // ROW_CHUNKS
    img_copies, kv_copies = [], []
    for i in range(ROW_CHUNKS):
        cut = pl.ds(i * step, step)
        c = pltpu.make_async_copy(images.at[:, :, cut], x_s.at[:, :, cut], img_sem.at[i])
        c.start()
        img_copies.append(c)
        c = pltpu.make_async_copy(
            w_qkv.at[cut, pl.ds(side, 2 * side)], w_s.at[cut, pl.ds(side, 2 * side)], in_sem.at[i]
        )
        c.start()
        kv_copies.append(c)
    small = []
    pairs = [(b_qkv, b_s), (q_gain, qg_s), (k_gain, kg_s), (key_basis, kb_s), (value_basis, vb_s), (centers, cen_s)]
    for i, (src, dst) in enumerate(pairs):
        c = pltpu.make_async_copy(src, dst, small_sem.at[i])
        c.start()
        small.append(c)
    q_copy = pltpu.make_async_copy(
        w_qkv.at[:, pl.ds(0, side)], w_s.at[:, pl.ds(0, side)], in_sem.at[ROW_CHUNKS]
    )
    q_copy.start()

    for c in small:
        c.wait()
    kbd[...] = jnp.zeros_like(kbd)
    vbd[...] = jnp.zeros_like(vbd)
    for h in range(heads):
        kbd[h * rank:(h + 1) * rank, h * head_dim:(h + 1) * head_dim] = kb_s[h]
        vbd[h * rank:(h + 1) * rank, h * head_dim:(h + 1) * head_dim] = vb_s[h]

    for i in range(ROW_CHUNKS):
        img_copies[i].wait()
        kv_copies[i].wait()
        piece = jnp.dot(
            x_s[:, :, i * step:(i + 1) * step].reshape(rows, step),
            w_s[i * step:(i + 1) * step, side:3 * side],
            preferred_element_type=jnp.float32,
        )
        if i == 0:
            kv_acc[...] = piece
        else:
            kv_acc[...] += piece

    def gain_row(ref):
        return ref[...].reshape(1, head_dim)

    def bias_row(column):
        return b_s[pl.ds(column, head_dim)].reshape(1, head_dim)

    part[0] = jnp.zeros_like(part[0])
    for h in range(heads):
        cut = slice(h * head_dim, (h + 1) * head_dim)
        raw = kv_acc[:, cut] + bias_row(side + h * head_dim)
        mean_square = jnp.mean(raw * raw, axis=-1, keepdims=True)
        keys = raw * lax.rsqrt(mean_square + epsilon) * gain_row(kg_s)
        vcut = slice(side + h * head_dim, side + (h + 1) * head_dim)
        values = kv_acc[:, vcut] + bias_row(2 * side + h * head_dim)
        for b in range(samples):
            own_rows = slice(b * tokens, (b + 1) * tokens)
            for j, one in enumerate((keys, values)):
                line = (b * 2 + j) * heads + h
                part[0, line:line + 1, :] = jnp.sum(one[own_rows], axis=0, keepdims=True)
            kc_s[own_rows, cut] = keys[own_rows] - cen_s[b, h, 0:1, :]
            vc_s[own_rows, cut] = values[own_rows] - cen_s[b, h, 1:2, :]

    pl.semaphore_wait(barrier, len(greeted))
    started = []

    def send(src, dst, send_sem, recv_sem, device):
        c = pltpu.make_async_remote_copy(
            src_ref=src, dst_ref=dst, send_sem=send_sem, recv_sem=recv_sem,
            device_id={"seq": device}, device_id_type=MESH,
        )
        c.start()
        started.append(c)
        return c

    def goes(direction, distance, b):
        if distance < half or chips % 2:
            return True
        return (b < samples // 2) == (direction == 0)

    rights, lefts, sib_owns, sib_lefts, sib_rights = {}, {}, {}, {}, {}

    def send_right(distance, b):
        if distance <= half and goes(0, distance, b):
            src = own.at[b] if distance == 1 else left_in.at[distance - 2, b]
            rights[distance, b] = send(
                src, left_in.at[distance - 1, b], right_send.at[distance - 1, b],
                right_recv.at[distance - 1, b], right,
            )

    def send_left(distance, b):
        if distance <= half and goes(1, distance, b):
            src = own.at[b] if distance == 1 else right_in.at[distance - 2, b]
            lefts[distance, b] = send(
                src, right_in.at[distance - 1, b], left_send.at[distance - 1, b],
                left_recv.at[distance - 1, b], left,
            )

    for b in range(samples):
        own_rows = slice(b * tokens, (b + 1) * tokens)
        for j, (src, basis) in enumerate(((kc_s, kbd), (vc_s, vbd))):
            coded = lax.dot_general(
                basis[:codes, :], src[own_rows, :], NT, precision=highest,
                preferred_element_type=jnp.float32,
            )
            own[b, j * codes:(j + 1) * codes, :] = coded.astype(jnp.bfloat16)
        send_right(1, b)
        send_left(1, b)
        sib_owns[b] = send(own.at[b], sib_own.at[b], so_send.at[b], so_recv.at[b], sibling)

    exchanges = []

    def exchange(level):
        if level > 0:
            exchanges[level - 1].wait_recv()
            part[level] = part[level - 1] + part_in[level - 1]
        if level < levels:
            exchanges.append(
                send(part.at[level], part_in.at[level], p_send.at[level], p_recv.at[level], partners[level])
            )

    exchange(0)

    q_copy.wait()
    q_acc[...] = jnp.dot(
        x_s[...].reshape(rows, width), w_s[:, :side], preferred_element_type=jnp.float32
    )
    scale = math.log2(math.e) / math.sqrt(head_dim)
    for h in range(heads):
        cut = slice(h * head_dim, (h + 1) * head_dim)
        raw = q_acc[:, cut] + bias_row(h * head_dim)
        mean_square = jnp.mean(raw * raw, axis=-1, keepdims=True)
        query = raw * lax.rsqrt(mean_square + epsilon) * gain_row(qg_s) * scale
        qs_s[:, cut] = query
        coded = lax.dot_general(
            query, kbd[:, cut], NT, precision=highest, preferred_element_type=jnp.float32
        )
        high = coded.astype(jnp.bfloat16)
        low = (coded - high.astype(jnp.float32)).astype(jnp.bfloat16)
        for b in range(samples):
            own_rows = slice(b * tokens, (b + 1) * tokens)
            qbd[b, h * tokens:(h + 1) * tokens, :LANES] = high[own_rows]
            qbd[b, h * tokens:(h + 1) * tokens, LANES:] = low[own_rows]

    def near(b):
        own_rows = slice(b * tokens, (b + 1) * tokens)
        for h in range(heads):
            cut = slice(h * head_dim, (h + 1) * head_dim)
            lines = slice(h * tokens, (h + 1) * tokens)
            scores = lax.dot_general(
                qs_s[own_rows, cut], kc_s[own_rows, cut], NT, precision=highest,
                preferred_element_type=jnp.float32,
            )
            top = jnp.max(scores, axis=-1, keepdims=True)
            weights = jnp.exp2(scores - top)
            total = jnp.sum(weights, axis=-1, keepdims=True)
            wide = jnp.broadcast_to(top, (tokens, LANES))
            m_s[b, lines, :] = wide
            mn_s[b, lines, :] = wide
            ln_s[b, lines, :] = jnp.broadcast_to(total, (tokens, LANES))
            accn_s[b, lines, :] = jnp.dot(
                weights, vc_s[own_rows, cut], precision=highest, preferred_element_type=jnp.float32
            )
        acc_s[b] = jnp.zeros_like(acc_s[b])

    def absorb(b, blocks):
        key_side = jnp.concatenate([r[:LANES, :] for r in blocks], axis=1)
        scores = jnp.dot(
            qbd[b], jnp.concatenate([key_side, key_side], axis=0), preferred_element_type=jnp.float32
        )
        before = m_s[b]
        now = jnp.maximum(before, jnp.max(scores, axis=-1, keepdims=True))
        weights = jnp.exp2(scores - now[:, :1]).astype(jnp.bfloat16)
        value_side = jnp.concatenate([r[codes:2 * codes, :] for r in blocks], axis=1)
        ones = jnp.ones((LANES - codes, value_side.shape[1]), jnp.bfloat16)
        added = lax.dot_general(
            weights, jnp.concatenate([value_side, ones], axis=0), NT, preferred_element_type=jnp.float32
        )
        acc_s[b] = acc_s[b] * jnp.exp2(before - now) + added
        m_s[b] = now

    for b in range(samples):
        near(b)

    waiting = {b: [] for b in range(samples)}
    for distance in range(1, half + 1):
        for b in range(samples):
            blocks = []
            if (distance, b) in rights:
                rights[distance, b].wait_recv()
                send_right(distance + 1, b)
                src = left_in.at[distance - 1, b]
                sib_lefts[distance, b] = send(
                    src, sib_left.at[distance - 1, b], sl_send.at[distance - 1, b],
                    sl_recv.at[distance - 1, b], sibling,
                )
                blocks.append(src)
            if (distance, b) in lefts:
                lefts[distance, b].wait_recv()
                send_left(distance + 1, b)
                src = right_in.at[distance - 1, b]
                sib_rights[distance, b] = send(
                    src, sib_right.at[distance - 1, b], sr_send.at[distance - 1, b],
                    sr_recv.at[distance - 1, b], sibling,
                )
                blocks.append(src)
            if distance == 1:
                sib_owns[b].wait_recv()
                blocks.append(sib_own.at[b])
            else:
                for copies, held in ((sib_lefts, sib_left), (sib_rights, sib_right)):
                    if (distance - 1, b) in copies:
                        copies[distance - 1, b].wait_recv()
                        blocks.append(held.at[distance - 2, b])
            absorb(b, blocks)
        if distance <= levels:
            exchange(distance)
    for level in range(half + 1, levels + 1):
        exchange(level)
    sums[...] = part[levels]

    for b in range(samples):
        own_rows = slice(b * tokens, (b + 1) * tokens)
        blocks = []
        for copies, held in ((sib_lefts, sib_left), (sib_rights, sib_right)):
            if (half, b) in copies:
                copies[half, b].wait_recv()
                blocks.append(held.at[half - 1, b])
        absorb(b, blocks)
        for h in range(heads):
            cut = slice(h * head_dim, (h + 1) * head_dim)
            lines = slice(h * tokens, (h + 1) * tokens)
            gathered = acc_s[b, lines, :]
            fade = jnp.exp2(mn_s[b, lines, :] - m_s[b, lines, :])
            total = gathered[:, codes:codes + 1] + (fade * ln_s[b, lines, :])[:, :1]
            rebuilt = jnp.dot(
                gathered, vbd[:, cut], precision=highest, preferred_element_type=jnp.float32
            )
            result = (rebuilt + fade * accn_s[b, lines, :]) / total + cen_s[b, h, 1:2, :]
            attended[own_rows, cut] = result.astype(jnp.bfloat16)
    for c in started:
        c.wait_send()


def finish_kernel(length, refresh, attended, w_out, sums, centers, mixed, new_centers, tiles, sem):
    samples, heads, pair, head_dim = new_centers.shape
    count, _, _, tile = tiles.shape
    copies = []
    for n in range(count):
        cut = slice(n * tile, (n + 1) * tile)
        product = jnp.dot(attended[...], w_out[:, cut], preferred_element_type=jnp.float32)
        tiles[n] = product.astype(jnp.bfloat16).reshape(tiles.shape[1:])
        c = pltpu.make_async_copy(tiles.at[n], mixed.at[:, :, pl.ds(n * tile, tile)], sem.at[n])
        c.start()
        copies.append(c)
    for b in range(samples):
        for j in range(pair):
            for h in range(heads):
                line = (b * pair + j) * heads + h
                fresh = sums[line:line + 1, :] / length
                old = centers[b, h, j:j + 1, :]
                new_centers[b, h, j:j + 1, :] = jnp.where(refresh[j, h] == 1, fresh, old)
    for c in copies:
        c.wait()


def per_device(
    seq_count, natural,
    images, w_qkv, b_qkv, q_gain, k_gain, key_basis, value_basis, centers, refresh, w_out
):
    samples, tokens, width = images.shape
    heads, head_dim, rank = key_basis.shape
    key_basis = jnp.swapaxes(key_basis, 1, 2)
    value_basis = jnp.swapaxes(value_basis, 1, 2)
    centers = jnp.transpose(centers, (0, 2, 1, 3))
    side = heads * head_dim
    rows = samples * tokens
    codes = heads * rank
    chips = seq_count // 2
    half = chips // 2
    levels = seq_count.bit_length() - 1
    lines = -(-samples * 2 * heads // 8) * 8
    f32, bf16 = jnp.float32, jnp.bfloat16
    hbm_spec = pl.BlockSpec(memory_space=pltpu.HBM)
    vmem_spec = pl.BlockSpec(memory_space=pltpu.VMEM)
    dma = pltpu.SemaphoreType.DMA
    block = (samples, 2 * codes, tokens)
    stat = pltpu.VMEM((samples, heads * tokens, LANES), f32)
    attended, sums = pl.pallas_call(
        functools.partial(attend_kernel, seq_count, natural),
        out_shape=(
            jax.ShapeDtypeStruct((rows, side), bf16),
            jax.ShapeDtypeStruct((lines, head_dim), f32),
        ),
        in_specs=[hbm_spec] * 8,
        out_specs=(vmem_spec, vmem_spec),
        scratch_shapes=[
            pltpu.VMEM(images.shape, bf16),
            pltpu.VMEM(w_qkv.shape, bf16),
            pltpu.VMEM(b_qkv.shape, f32),
            pltpu.VMEM(q_gain.shape, f32),
            pltpu.VMEM(k_gain.shape, f32),
            pltpu.VMEM(key_basis.shape, f32),
            pltpu.VMEM(value_basis.shape, f32),
            pltpu.VMEM(centers.shape, f32),
            pltpu.VMEM((rows, 2 * side), f32),
            pltpu.VMEM((rows, side), f32),
            pltpu.VMEM((LANES, side), f32),
            pltpu.VMEM((LANES, side), f32),
            pltpu.VMEM((rows, side), f32),
            pltpu.VMEM((rows, side), f32),
            pltpu.VMEM((rows, side), f32),
            pltpu.VMEM((samples, heads * tokens, 2 * LANES), bf16),
            stat, stat, stat, stat, stat,
            pltpu.VMEM(block, bf16),
            pltpu.VMEM((half,) + block, bf16),
            pltpu.VMEM((half,) + block, bf16),
            pltpu.VMEM(block, bf16),
            pltpu.VMEM((half,) + block, bf16),
            pltpu.VMEM((half,) + block, bf16),
            pltpu.VMEM((levels + 1, lines, head_dim), f32),
            pltpu.VMEM((levels, lines, head_dim), f32),
            dma((ROW_CHUNKS + 1,)), dma((ROW_CHUNKS,)), dma((6,)),
            dma((half, samples)), dma((half, samples)), dma((half, samples)), dma((half, samples)),
            dma((samples,)), dma((samples,)),
            dma((half, samples)), dma((half, samples)), dma((half, samples)), dma((half, samples)),
            dma((levels,)), dma((levels,)),
        ],
        compiler_params=pltpu.CompilerParams(
            collective_id=0, has_side_effects=True, vmem_limit_bytes=40 << 20
        ),
        name="attend",
    )(*[
        pltpu.with_memory_space_constraint(a, pltpu.HBM)
        for a in (images, w_qkv, b_qkv, q_gain, k_gain, key_basis, value_basis, centers)
    ])

    tile = width // OUT_TILES
    mixed, new_centers = pl.pallas_call(
        functools.partial(finish_kernel, float(tokens * seq_count)),
        out_shape=(
            jax.ShapeDtypeStruct(images.shape, bf16),
            jax.ShapeDtypeStruct(centers.shape, f32),
        ),
        in_specs=[pl.BlockSpec(memory_space=pltpu.SMEM)] + [vmem_spec] * 4,
        out_specs=(hbm_spec, vmem_spec),
        scratch_shapes=[
            pltpu.VMEM((OUT_TILES, samples, tokens, tile), bf16),
            dma((OUT_TILES,)),
        ],
        compiler_params=pltpu.CompilerParams(vmem_limit_bytes=16 << 20),
        name="finish",
    )(refresh, attended, w_out, sums, centers)
    return mixed, jnp.transpose(new_centers, (0, 2, 1, 3))


def solution(mesh):
    return jax.shard_map(
        functools.partial(per_device, mesh.shape["seq"], natural_ring(mesh)),
        mesh=mesh,
        in_specs=(
            P("groups", "seq", None),
            P(),
            P(),
            P(),
            P(),
            P(),
            P(),
            P("groups", None, None, None),
            P(),
            P(),
        ),
        out_specs=(P("groups", "seq", None), P("groups", None, None, None)),
        check_vma=False,
    )
```

```python
import functools
import math

import jax
import jax.numpy as jnp
from jax import lax
from jax.experimental import pallas as pl
from jax.experimental.pallas import tpu as pltpu
from jax.sharding import PartitionSpec as P

epsilon = 1e-06
highest = lax.Precision.HIGH
LANES = 128
ROW_CHUNKS = 6
OUT_TILES = 6
MESH = pl.DeviceIdType.MESH
NT = (((1,), (1,)), ((), ()))


def natural_ring(mesh):
    try:
        names = list(mesh.axis_names)
        line = mesh.devices
        if names.index("seq") == 0:
            line = line.T
        chips = [d.coords for d in line[0][::2]]
        return all(
            sum(abs(a - b) for a, b in zip(one, two)) == 1 for one, two in zip(chips, chips[1:])
        )
    except Exception:
        return False


def attend_kernel(
    seq_count, natural,
    images, w_qkv, b_qkv, q_gain, k_gain, key_basis, value_basis, centers,
    attended, sums,
    x_s, w_s, b_s, qg_s, kg_s, kb_s, vb_s, cen_s,
    kv_acc, q_acc, kbd, vbd, kc_s, vc_s, qs_s, qbd,
    m_s, mn_s, ln_s, accn_s, acc_s,
    own, left_in, right_in, sib_own, sib_left, sib_right, part, part_in,
    in_sem, img_sem, small_sem,
    right_send, right_recv, left_send, left_recv,
    so_send, so_recv, sl_send, sl_recv, sr_send, sr_recv, p_send, p_recv,
):
    samples, tokens, width = x_s.shape
    heads, rank, head_dim = kb_s.shape
    codes = heads * rank
    side = heads * head_dim
    rows = samples * tokens
    chips = seq_count // 2
    half = chips // 2
    levels = seq_count.bit_length() - 1
    me = lax.axis_index("seq")
    core = me % 2
    chip = me // 2

    if natural:
        right_chip = (chip + 1) % chips
        left_chip = (chip + chips - 1) % chips
    else:
        def chip_at(pos):
            back = pos // half
            z = (1 - back) * pos + back * (chips - 1 - pos)
            return 2 * z + back

        far = chip % 2
        pos = (1 - far) * (chip // 2) + far * (chips - 1 - chip // 2)
        right_chip = chip_at((pos + 1) % chips)
        left_chip = chip_at((pos + chips - 1) % chips)
    right = right_chip * 2 + core
    left = left_chip * 2 + core
    sibling = chip * 2 + 1 - core
    partners = [me + bit * (1 - 2 * ((me // bit) % 2)) for bit in [1 << k for k in range(levels)]]

    barrier = pltpu.get_barrier_semaphore()
    greeted = [right, left] + partners
    for device in greeted:
        pl.semaphore_signal(barrier, inc=1, device_id={"seq": device}, device_id_type=MESH)

    small = []
    pairs = [(b_qkv, b_s), (q_gain, qg_s), (k_gain, kg_s), (key_basis, kb_s), (value_basis, vb_s), (centers, cen_s)]
    for i, (src, dst) in enumerate(pairs):
        c = pltpu.make_async_copy(src, dst, small_sem.at[i])
        c.start()
        small.append(c)
    step = width // ROW_CHUNKS
    img_copies, kv_copies = [], []
    for i in range(ROW_CHUNKS):
        cut = pl.ds(i * step, step)
        c = pltpu.make_async_copy(images.at[:, :, cut], x_s.at[:, :, cut], img_sem.at[i])
        c.start()
        img_copies.append(c)
        c = pltpu.make_async_copy(
            w_qkv.at[cut, pl.ds(side, 2 * side)], w_s.at[cut, pl.ds(side, 2 * side)], in_sem.at[i]
        )
        c.start()
        kv_copies.append(c)
    q_copy = pltpu.make_async_copy(
        w_qkv.at[:, pl.ds(0, side)], w_s.at[:, pl.ds(0, side)], in_sem.at[ROW_CHUNKS]
    )
    q_copy.start()

    for c in small:
        c.wait()
    kbd[...] = jnp.zeros_like(kbd)
    vbd[...] = jnp.zeros_like(vbd)
    for h in range(heads):
        kbd[h * rank:(h + 1) * rank, h * head_dim:(h + 1) * head_dim] = kb_s[h]
        vbd[h * rank:(h + 1) * rank, h * head_dim:(h + 1) * head_dim] = vb_s[h]

    for i in range(ROW_CHUNKS):
        img_copies[i].wait()
        kv_copies[i].wait()
        piece = jnp.dot(
            x_s[:, :, i * step:(i + 1) * step].reshape(rows, step),
            w_s[i * step:(i + 1) * step, side:3 * side],
            preferred_element_type=jnp.float32,
        )
        if i == 0:
            kv_acc[...] = piece
        else:
            kv_acc[...] += piece

    def gain_row(ref):
        return ref[...].reshape(1, head_dim)

    def bias_row(column):
        return b_s[pl.ds(column, head_dim)].reshape(1, head_dim)

    part[0] = jnp.zeros_like(part[0])
    for h in range(heads):
        cut = slice(h * head_dim, (h + 1) * head_dim)
        raw = kv_acc[:, cut] + bias_row(side + h * head_dim)
        mean_square = jnp.mean(raw * raw, axis=-1, keepdims=True)
        keys = raw * lax.rsqrt(mean_square + epsilon) * gain_row(kg_s)
        vcut = slice(side + h * head_dim, side + (h + 1) * head_dim)
        values = kv_acc[:, vcut] + bias_row(2 * side + h * head_dim)
        for b in range(samples):
            own_rows = slice(b * tokens, (b + 1) * tokens)
            for j, one in enumerate((keys, values)):
                line = (b * 2 + j) * heads + h
                part[0, line:line + 1, :] = jnp.sum(one[own_rows], axis=0, keepdims=True)
            kc_s[own_rows, cut] = keys[own_rows] - cen_s[b, h, 0:1, :]
            vc_s[own_rows, cut] = values[own_rows] - cen_s[b, h, 1:2, :]

    pl.semaphore_wait(barrier, len(greeted))
    started = []

    def send(src, dst, send_sem, recv_sem, device):
        c = pltpu.make_async_remote_copy(
            src_ref=src, dst_ref=dst, send_sem=send_sem, recv_sem=recv_sem,
            device_id={"seq": device}, device_id_type=MESH,
        )
        c.start()
        started.append(c)
        return c

    def goes(direction, distance, b):
        if distance < half or chips % 2:
            return True
        return (b < samples // 2) == (direction == 0)

    rights, lefts, sib_owns, sib_lefts, sib_rights = {}, {}, {}, {}, {}

    def send_right(distance, b):
        if distance <= half and goes(0, distance, b):
            src = own.at[b] if distance == 1 else left_in.at[distance - 2, b]
            rights[distance, b] = send(
                src, left_in.at[distance - 1, b], right_send.at[distance - 1, b],
                right_recv.at[distance - 1, b], right,
            )

    def send_left(distance, b):
        if distance <= half and goes(1, distance, b):
            src = own.at[b] if distance == 1 else right_in.at[distance - 2, b]
            lefts[distance, b] = send(
                src, right_in.at[distance - 1, b], left_send.at[distance - 1, b],
                left_recv.at[distance - 1, b], left,
            )

    exchanges = []

    def exchange(level):
        if level > 0:
            exchanges[level - 1].wait_recv()
            part[level] = part[level - 1] + part_in[level - 1]
        if level < levels:
            exchanges.append(
                send(part.at[level], part_in.at[level], p_send.at[level], p_recv.at[level], partners[level])
            )

    exchange(0)

    for b in range(samples):
        own_rows = slice(b * tokens, (b + 1) * tokens)
        for j, (src, basis) in enumerate(((kc_s, kbd), (vc_s, vbd))):
            coded = lax.dot_general(
                basis[:codes, :], src[own_rows, :], NT, precision=highest,
                preferred_element_type=jnp.float32,
            )
            own[b, j * codes:(j + 1) * codes, :] = coded.astype(jnp.bfloat16)
        send_right(1, b)
        send_left(1, b)
        sib_owns[b] = send(own.at[b], sib_own.at[b], so_send.at[b], so_recv.at[b], sibling)

    q_copy.wait()
    q_acc[...] = jnp.dot(
        x_s[...].reshape(rows, width), w_s[:, :side], preferred_element_type=jnp.float32
    )
    scale = math.log2(math.e) / math.sqrt(head_dim)
    for h in range(heads):
        cut = slice(h * head_dim, (h + 1) * head_dim)
        raw = q_acc[:, cut] + bias_row(h * head_dim)
        mean_square = jnp.mean(raw * raw, axis=-1, keepdims=True)
        query = raw * lax.rsqrt(mean_square + epsilon) * gain_row(qg_s) * scale
        qs_s[:, cut] = query
        coded = lax.dot_general(
            query, kbd[:, cut], NT, precision=highest, preferred_element_type=jnp.float32
        )
        high = coded.astype(jnp.bfloat16)
        low = (coded - high.astype(jnp.float32)).astype(jnp.bfloat16)
        for b in range(samples):
            own_rows = slice(b * tokens, (b + 1) * tokens)
            qbd[b, h * tokens:(h + 1) * tokens, :LANES] = high[own_rows]
            qbd[b, h * tokens:(h + 1) * tokens, LANES:] = low[own_rows]

    def near(b):
        own_rows = slice(b * tokens, (b + 1) * tokens)
        for h in range(heads):
            cut = slice(h * head_dim, (h + 1) * head_dim)
            lines = slice(h * tokens, (h + 1) * tokens)
            scores = lax.dot_general(
                qs_s[own_rows, cut], kc_s[own_rows, cut], NT, precision=highest,
                preferred_element_type=jnp.float32,
            )
            top = jnp.max(scores, axis=-1, keepdims=True)
            weights = jnp.exp2(scores - top)
            total = jnp.sum(weights, axis=-1, keepdims=True)
            wide = jnp.broadcast_to(top, (tokens, LANES))
            m_s[b, lines, :] = wide
            mn_s[b, lines, :] = wide
            ln_s[b, lines, :] = jnp.broadcast_to(total, (tokens, LANES))
            accn_s[b, lines, :] = jnp.dot(
                weights, vc_s[own_rows, cut], precision=highest, preferred_element_type=jnp.float32
            )
        acc_s[b] = jnp.zeros_like(acc_s[b])

    def absorb(b, blocks):
        key_side = jnp.concatenate([r[:LANES, :] for r in blocks], axis=1)
        scores = jnp.dot(
            qbd[b], jnp.concatenate([key_side, key_side], axis=0), preferred_element_type=jnp.float32
        )
        before = m_s[b]
        now = jnp.maximum(before, jnp.max(scores, axis=-1, keepdims=True))
        weights = jnp.exp2(scores - now[:, :1]).astype(jnp.bfloat16)
        value_side = jnp.concatenate([r[codes:2 * codes, :] for r in blocks], axis=1)
        ones = jnp.ones((LANES - codes, value_side.shape[1]), jnp.bfloat16)
        added = lax.dot_general(
            weights, jnp.concatenate([value_side, ones], axis=0), NT, preferred_element_type=jnp.float32
        )
        acc_s[b] = acc_s[b] * jnp.exp2(before - now) + added
        m_s[b] = now

    def pass_on(distance):
        for b in range(samples):
            if (distance, b) in rights:
                rights[distance, b].wait_recv()
                send_right(distance + 1, b)
                sib_lefts[distance, b] = send(
                    left_in.at[distance - 1, b], sib_left.at[distance - 1, b],
                    sl_send.at[distance - 1, b], sl_recv.at[distance - 1, b], sibling,
                )
            if (distance, b) in lefts:
                lefts[distance, b].wait_recv()
                send_left(distance + 1, b)
                sib_rights[distance, b] = send(
                    right_in.at[distance - 1, b], sib_right.at[distance - 1, b],
                    sr_send.at[distance - 1, b], sr_recv.at[distance - 1, b], sibling,
                )

    def absorb_stage(distance):
        for b in range(samples):
            blocks = []
            if (distance, b) in rights:
                blocks.append(left_in.at[distance - 1, b])
            if (distance, b) in lefts:
                blocks.append(right_in.at[distance - 1, b])
            if distance == 1:
                sib_owns[b].wait_recv()
                blocks.append(sib_own.at[b])
            else:
                for copies, held in ((sib_lefts, sib_left), (sib_rights, sib_right)):
                    if (distance - 1, b) in copies:
                        copies[distance - 1, b].wait_recv()
                        blocks.append(held.at[distance - 2, b])
            absorb(b, blocks)

    exchange(1)
    for distance in range(1, half + 1):
        pass_on(distance)
        if distance == 1:
            for b in range(samples):
                near(b)
        else:
            absorb_stage(distance - 1)
        if distance + 1 <= levels:
            exchange(distance + 1)
    absorb_stage(half)
    for level in range(half + 2, levels + 1):
        exchange(level)
    sums[...] = part[levels]

    for b in range(samples):
        own_rows = slice(b * tokens, (b + 1) * tokens)
        blocks = []
        for copies, held in ((sib_lefts, sib_left), (sib_rights, sib_right)):
            if (half, b) in copies:
                copies[half, b].wait_recv()
                blocks.append(held.at[half - 1, b])
        absorb(b, blocks)
        for h in range(heads):
            cut = slice(h * head_dim, (h + 1) * head_dim)
            lines = slice(h * tokens, (h + 1) * tokens)
            gathered = acc_s[b, lines, :]
            fade = jnp.exp2(mn_s[b, lines, :] - m_s[b, lines, :])
            total = gathered[:, codes:codes + 1] + (fade * ln_s[b, lines, :])[:, :1]
            rebuilt = jnp.dot(
                gathered, vbd[:, cut], precision=highest, preferred_element_type=jnp.float32
            )
            result = (rebuilt + fade * accn_s[b, lines, :]) / total + cen_s[b, h, 1:2, :]
            attended[own_rows, cut] = result.astype(jnp.bfloat16)
    for c in started:
        c.wait_send()


def finish_kernel(length, refresh, attended, w_out, sums, centers, mixed, new_centers, tiles, sem):
    samples, heads, pair, head_dim = new_centers.shape
    count, _, _, tile = tiles.shape
    copies = []
    for n in range(count):
        cut = slice(n * tile, (n + 1) * tile)
        product = jnp.dot(attended[...], w_out[:, cut], preferred_element_type=jnp.float32)
        tiles[n] = product.astype(jnp.bfloat16).reshape(tiles.shape[1:])
        c = pltpu.make_async_copy(tiles.at[n], mixed.at[:, :, pl.ds(n * tile, tile)], sem.at[n])
        c.start()
        copies.append(c)
    for b in range(samples):
        for j in range(pair):
            for h in range(heads):
                line = (b * pair + j) * heads + h
                fresh = sums[line:line + 1, :] / length
                old = centers[b, h, j:j + 1, :]
                new_centers[b, h, j:j + 1, :] = jnp.where(refresh[j, h] == 1, fresh, old)
    for c in copies:
        c.wait()


def per_device(
    seq_count, natural,
    images, w_qkv, b_qkv, q_gain, k_gain, key_basis, value_basis, centers, refresh, w_out
):
    samples, tokens, width = images.shape
    heads, head_dim, rank = key_basis.shape
    key_basis = jnp.swapaxes(key_basis, 1, 2)
    value_basis = jnp.swapaxes(value_basis, 1, 2)
    centers = jnp.transpose(centers, (0, 2, 1, 3))
    side = heads * head_dim
    rows = samples * tokens
    codes = heads * rank
    chips = seq_count // 2
    half = chips // 2
    levels = seq_count.bit_length() - 1
    lines = -(-samples * 2 * heads // 8) * 8
    f32, bf16 = jnp.float32, jnp.bfloat16
    hbm_spec = pl.BlockSpec(memory_space=pltpu.HBM)
    vmem_spec = pl.BlockSpec(memory_space=pltpu.VMEM)
    dma = pltpu.SemaphoreType.DMA
    block = (samples, 2 * codes, tokens)
    stat = pltpu.VMEM((samples, heads * tokens, LANES), f32)
    attended, sums = pl.pallas_call(
        functools.partial(attend_kernel, seq_count, natural),
        out_shape=(
            jax.ShapeDtypeStruct((rows, side), bf16),
            jax.ShapeDtypeStruct((lines, head_dim), f32),
        ),
        in_specs=[hbm_spec] * 8,
        out_specs=(vmem_spec, vmem_spec),
        scratch_shapes=[
            pltpu.VMEM(images.shape, bf16),
            pltpu.VMEM(w_qkv.shape, bf16),
            pltpu.VMEM(b_qkv.shape, f32),
            pltpu.VMEM(q_gain.shape, f32),
            pltpu.VMEM(k_gain.shape, f32),
            pltpu.VMEM(key_basis.shape, f32),
            pltpu.VMEM(value_basis.shape, f32),
            pltpu.VMEM(centers.shape, f32),
            pltpu.VMEM((rows, 2 * side), f32),
            pltpu.VMEM((rows, side), f32),
            pltpu.VMEM((LANES, side), f32),
            pltpu.VMEM((LANES, side), f32),
            pltpu.VMEM((rows, side), f32),
            pltpu.VMEM((rows, side), f32),
            pltpu.VMEM((rows, side), f32),
            pltpu.VMEM((samples, heads * tokens, 2 * LANES), bf16),
            stat, stat, stat, stat, stat,
            pltpu.VMEM(block, bf16),
            pltpu.VMEM((half,) + block, bf16),
            pltpu.VMEM((half,) + block, bf16),
            pltpu.VMEM(block, bf16),
            pltpu.VMEM((half,) + block, bf16),
            pltpu.VMEM((half,) + block, bf16),
            pltpu.VMEM((levels + 1, lines, head_dim), f32),
            pltpu.VMEM((levels, lines, head_dim), f32),
            dma((ROW_CHUNKS + 1,)), dma((ROW_CHUNKS,)), dma((6,)),
            dma((half, samples)), dma((half, samples)), dma((half, samples)), dma((half, samples)),
            dma((samples,)), dma((samples,)),
            dma((half, samples)), dma((half, samples)), dma((half, samples)), dma((half, samples)),
            dma((levels,)), dma((levels,)),
        ],
        compiler_params=pltpu.CompilerParams(
            collective_id=0, has_side_effects=True, vmem_limit_bytes=40 << 20
        ),
        name="attend",
    )(*[
        pltpu.with_memory_space_constraint(a, pltpu.HBM)
        for a in (images, w_qkv, b_qkv, q_gain, k_gain, key_basis, value_basis, centers)
    ])

    tile = width // OUT_TILES
    mixed, new_centers = pl.pallas_call(
        functools.partial(finish_kernel, float(tokens * seq_count)),
        out_shape=(
            jax.ShapeDtypeStruct(images.shape, bf16),
            jax.ShapeDtypeStruct(centers.shape, f32),
        ),
        in_specs=[pl.BlockSpec(memory_space=pltpu.SMEM)] + [vmem_spec] * 4,
        out_specs=(hbm_spec, vmem_spec),
        scratch_shapes=[
            pltpu.VMEM((OUT_TILES, samples, tokens, tile), bf16),
            dma((OUT_TILES,)),
        ],
        compiler_params=pltpu.CompilerParams(vmem_limit_bytes=16 << 20),
        name="finish",
    )(refresh, attended, w_out, sums, centers)
    return mixed, jnp.transpose(new_centers, (0, 2, 1, 3))


def solution(mesh):
    return jax.shard_map(
        functools.partial(per_device, mesh.shape["seq"], natural_ring(mesh)),
        mesh=mesh,
        in_specs=(
            P("groups", "seq", None),
            P(),
            P(),
            P(),
            P(),
            P(),
            P(),
            P("groups", None, None, None),
            P(),
            P(),
        ),
        out_specs=(P("groups", "seq", None), P("groups", None, None, None)),
        check_vma=False,
    )
```

```python
import functools
import math

import jax
import jax.numpy as jnp
from jax import lax
from jax.experimental import pallas as pl
from jax.experimental.pallas import tpu as pltpu
from jax.sharding import PartitionSpec as P

epsilon = 1e-06
highest = lax.Precision.HIGH
LANES = 128
ROW_CHUNKS = 6
OUT_TILES = 6
MESH = pl.DeviceIdType.MESH
NT = (((1,), (1,)), ((), ()))


def natural_ring(mesh):
    try:
        names = list(mesh.axis_names)
        line = mesh.devices
        if names.index("seq") == 0:
            line = line.T
        chips = [d.coords for d in line[0][::2]]
        return all(
            sum(abs(a - b) for a, b in zip(one, two)) == 1 for one, two in zip(chips, chips[1:])
        )
    except Exception:
        return False


def attend_kernel(
    seq_count, natural,
    images, w_qkv, b_qkv, q_gain, k_gain, key_basis, value_basis, centers,
    attended, sums,
    x_s, w_s, b_s, qg_s, kg_s, kb_s, vb_s, cen_s,
    kv_acc, q_acc, kbd, vbd, kc_s, vc_s, qs_s, qbd,
    m_s, mn_s, ln_s, accn_s, acc_s,
    own, left_in, right_in, sib_own, sib_left, sib_right, part, part_in,
    in_sem, img_sem, small_sem,
    right_send, right_recv, left_send, left_recv,
    so_send, so_recv, sl_send, sl_recv, sr_send, sr_recv, p_send, p_recv,
):
    samples, tokens, width = x_s.shape
    heads, rank, head_dim = kb_s.shape
    codes = heads * rank
    side = heads * head_dim
    rows = samples * tokens
    chips = seq_count // 2
    half = chips // 2
    levels = seq_count.bit_length() - 1
    me = lax.axis_index("seq")
    core = me % 2
    chip = me // 2

    if natural:
        right_chip = (chip + 1) % chips
        left_chip = (chip + chips - 1) % chips
    else:
        def chip_at(pos):
            back = pos // half
            z = (1 - back) * pos + back * (chips - 1 - pos)
            return 2 * z + back

        far = chip % 2
        pos = (1 - far) * (chip // 2) + far * (chips - 1 - chip // 2)
        right_chip = chip_at((pos + 1) % chips)
        left_chip = chip_at((pos + chips - 1) % chips)
    right = right_chip * 2 + core
    left = left_chip * 2 + core
    sibling = chip * 2 + 1 - core
    partners = [me + bit * (1 - 2 * ((me // bit) % 2)) for bit in [1 << k for k in range(levels)]]

    barrier = pltpu.get_barrier_semaphore()
    greeted = [right, left] + partners
    for device in greeted:
        pl.semaphore_signal(barrier, inc=1, device_id={"seq": device}, device_id_type=MESH)

    small = []
    pairs = [(b_qkv, b_s), (q_gain, qg_s), (k_gain, kg_s), (key_basis, kb_s), (value_basis, vb_s), (centers, cen_s)]
    for i, (src, dst) in enumerate(pairs):
        c = pltpu.make_async_copy(src, dst, small_sem.at[i])
        c.start()
        small.append(c)
    step = width // ROW_CHUNKS
    img_copies, kv_copies = [], []
    for i in range(ROW_CHUNKS):
        cut = pl.ds(i * step, step)
        c = pltpu.make_async_copy(images.at[:, :, cut], x_s.at[:, :, cut], img_sem.at[i])
        c.start()
        img_copies.append(c)
        c = pltpu.make_async_copy(
            w_qkv.at[cut, pl.ds(side, 2 * side)], w_s.at[cut, pl.ds(side, 2 * side)], in_sem.at[i]
        )
        c.start()
        kv_copies.append(c)
    q_copy = pltpu.make_async_copy(
        w_qkv.at[:, pl.ds(0, side)], w_s.at[:, pl.ds(0, side)], in_sem.at[ROW_CHUNKS]
    )
    q_copy.start()

    for c in small:
        c.wait()
    kbd[...] = jnp.zeros_like(kbd)
    vbd[...] = jnp.zeros_like(vbd)
    for h in range(heads):
        kbd[h * rank:(h + 1) * rank, h * head_dim:(h + 1) * head_dim] = kb_s[h]
        vbd[h * rank:(h + 1) * rank, h * head_dim:(h + 1) * head_dim] = vb_s[h]

    for i in range(ROW_CHUNKS):
        img_copies[i].wait()
        kv_copies[i].wait()
        piece = jnp.dot(
            x_s[:, :, i * step:(i + 1) * step].reshape(rows, step),
            w_s[i * step:(i + 1) * step, side:3 * side],
            preferred_element_type=jnp.float32,
        )
        if i == 0:
            kv_acc[...] = piece
        else:
            kv_acc[...] += piece

    def gain_row(ref):
        return ref[...].reshape(1, head_dim)

    def bias_row(column):
        return b_s[pl.ds(column, head_dim)].reshape(1, head_dim)

    part[0] = jnp.zeros_like(part[0])
    for h in range(heads):
        cut = slice(h * head_dim, (h + 1) * head_dim)
        raw = kv_acc[:, cut] + bias_row(side + h * head_dim)
        mean_square = jnp.mean(raw * raw, axis=-1, keepdims=True)
        keys = raw * lax.rsqrt(mean_square + epsilon) * gain_row(kg_s)
        vcut = slice(side + h * head_dim, side + (h + 1) * head_dim)
        values = kv_acc[:, vcut] + bias_row(2 * side + h * head_dim)
        for b in range(samples):
            own_rows = slice(b * tokens, (b + 1) * tokens)
            for j, one in enumerate((keys, values)):
                line = (b * 2 + j) * heads + h
                part[0, line:line + 1, :] = jnp.sum(one[own_rows], axis=0, keepdims=True)
            kc_s[own_rows, cut] = keys[own_rows] - cen_s[b, h, 0:1, :]
            vc_s[own_rows, cut] = values[own_rows] - cen_s[b, h, 1:2, :]

    pl.semaphore_wait(barrier, len(greeted))
    started = []

    def send(src, dst, send_sem, recv_sem, device):
        c = pltpu.make_async_remote_copy(
            src_ref=src, dst_ref=dst, send_sem=send_sem, recv_sem=recv_sem,
            device_id={"seq": device}, device_id_type=MESH,
        )
        c.start()
        started.append(c)
        return c

    def goes(direction, distance, b):
        if distance < half or chips % 2:
            return True
        return (b < samples // 2) == (direction == 0)

    rights, lefts, sib_owns, sib_lefts, sib_rights = {}, {}, {}, {}, {}

    def send_right(distance, b):
        if distance <= half and goes(0, distance, b):
            src = own.at[b] if distance == 1 else left_in.at[distance - 2, b]
            rights[distance, b] = send(
                src, left_in.at[distance - 1, b], right_send.at[distance - 1, b],
                right_recv.at[distance - 1, b], right,
            )

    def send_left(distance, b):
        if distance <= half and goes(1, distance, b):
            src = own.at[b] if distance == 1 else right_in.at[distance - 2, b]
            lefts[distance, b] = send(
                src, right_in.at[distance - 1, b], left_send.at[distance - 1, b],
                left_recv.at[distance - 1, b], left,
            )

    for b in range(samples):
        own_rows = slice(b * tokens, (b + 1) * tokens)
        for j, (src, basis) in enumerate(((kc_s, kbd), (vc_s, vbd))):
            coded = lax.dot_general(
                basis[:codes, :], src[own_rows, :], NT, precision=highest,
                preferred_element_type=jnp.float32,
            )
            own[b, j * codes:(j + 1) * codes, :] = coded.astype(jnp.bfloat16)
        send_right(1, b)
        send_left(1, b)
        sib_owns[b] = send(own.at[b], sib_own.at[b], so_send.at[b], so_recv.at[b], sibling)

    exchanges = []

    def exchange(level):
        if level > 0:
            exchanges[level - 1].wait_recv()
            part[level] = part[level - 1] + part_in[level - 1]
        if level < levels:
            exchanges.append(
                send(part.at[level], part_in.at[level], p_send.at[level], p_recv.at[level], partners[level])
            )

    exchange(0)

    q_copy.wait()
    q_acc[...] = jnp.dot(
        x_s[...].reshape(rows, width), w_s[:, :side], preferred_element_type=jnp.float32
    )
    scale = math.log2(math.e) / math.sqrt(head_dim)
    for h in range(heads):
        cut = slice(h * head_dim, (h + 1) * head_dim)
        raw = q_acc[:, cut] + bias_row(h * head_dim)
        mean_square = jnp.mean(raw * raw, axis=-1, keepdims=True)
        query = raw * lax.rsqrt(mean_square + epsilon) * gain_row(qg_s) * scale
        qs_s[:, cut] = query
        coded = lax.dot_general(
            query, kbd[:, cut], NT, precision=highest, preferred_element_type=jnp.float32
        )
        high = coded.astype(jnp.bfloat16)
        low = (coded - high.astype(jnp.float32)).astype(jnp.bfloat16)
        for b in range(samples):
            own_rows = slice(b * tokens, (b + 1) * tokens)
            qbd[b, h * tokens:(h + 1) * tokens, :LANES] = high[own_rows]
            qbd[b, h * tokens:(h + 1) * tokens, LANES:] = low[own_rows]

    def near(b):
        own_rows = slice(b * tokens, (b + 1) * tokens)
        for h in range(heads):
            cut = slice(h * head_dim, (h + 1) * head_dim)
            lines = slice(h * tokens, (h + 1) * tokens)
            scores = lax.dot_general(
                qs_s[own_rows, cut], kc_s[own_rows, cut], NT, precision=highest,
                preferred_element_type=jnp.float32,
            )
            top = jnp.max(scores, axis=-1, keepdims=True)
            weights = jnp.exp2(scores - top)
            total = jnp.sum(weights, axis=-1, keepdims=True)
            wide = jnp.broadcast_to(top, (tokens, LANES))
            m_s[b, lines, :] = wide
            mn_s[b, lines, :] = wide
            ln_s[b, lines, :] = jnp.broadcast_to(total, (tokens, LANES))
            accn_s[b, lines, :] = jnp.dot(
                weights, vc_s[own_rows, cut], precision=highest, preferred_element_type=jnp.float32
            )
        acc_s[b] = jnp.zeros_like(acc_s[b])

    def absorb(b, blocks):
        key_side = jnp.concatenate([r[:LANES, :] for r in blocks], axis=1)
        scores = jnp.dot(
            qbd[b], jnp.concatenate([key_side, key_side], axis=0), preferred_element_type=jnp.float32
        )
        before = m_s[b]
        now = jnp.maximum(before, jnp.max(scores, axis=-1, keepdims=True))
        weights = jnp.exp2(scores - now[:, :1]).astype(jnp.bfloat16)
        value_side = jnp.concatenate([r[codes:2 * codes, :] for r in blocks], axis=1)
        ones = jnp.ones((LANES - codes, value_side.shape[1]), jnp.bfloat16)
        added = lax.dot_general(
            weights, jnp.concatenate([value_side, ones], axis=0), NT, preferred_element_type=jnp.float32
        )
        acc_s[b] = acc_s[b] * jnp.exp2(before - now) + added
        m_s[b] = now

    for b in range(samples):
        near(b)

    waiting = {b: [] for b in range(samples)}
    for distance in range(1, half + 1):
        for b in range(samples):
            blocks = []
            if (distance, b) in rights:
                rights[distance, b].wait_recv()
                send_right(distance + 1, b)
                src = left_in.at[distance - 1, b]
                sib_lefts[distance, b] = send(
                    src, sib_left.at[distance - 1, b], sl_send.at[distance - 1, b],
                    sl_recv.at[distance - 1, b], sibling,
                )
                blocks.append(src)
            if (distance, b) in lefts:
                lefts[distance, b].wait_recv()
                send_left(distance + 1, b)
                src = right_in.at[distance - 1, b]
                sib_rights[distance, b] = send(
                    src, sib_right.at[distance - 1, b], sr_send.at[distance - 1, b],
                    sr_recv.at[distance - 1, b], sibling,
                )
                blocks.append(src)
            if distance == 1:
                sib_owns[b].wait_recv()
                blocks.append(sib_own.at[b])
            else:
                for copies, held in ((sib_lefts, sib_left), (sib_rights, sib_right)):
                    if (distance - 1, b) in copies:
                        copies[distance - 1, b].wait_recv()
                        blocks.append(held.at[distance - 2, b])
            absorb(b, blocks)
        if distance <= levels:
            exchange(distance)
    for level in range(half + 1, levels + 1):
        exchange(level)
    sums[...] = part[levels]

    for b in range(samples):
        own_rows = slice(b * tokens, (b + 1) * tokens)
        blocks = []
        for copies, held in ((sib_lefts, sib_left), (sib_rights, sib_right)):
            if (half, b) in copies:
                copies[half, b].wait_recv()
                blocks.append(held.at[half - 1, b])
        absorb(b, blocks)
        for h in range(heads):
            cut = slice(h * head_dim, (h + 1) * head_dim)
            lines = slice(h * tokens, (h + 1) * tokens)
            gathered = acc_s[b, lines, :]
            fade = jnp.exp2(mn_s[b, lines, :] - m_s[b, lines, :])
            total = gathered[:, codes:codes + 1] + (fade * ln_s[b, lines, :])[:, :1]
            rebuilt = jnp.dot(
                gathered, vbd[:, cut], precision=highest, preferred_element_type=jnp.float32
            )
            result = (rebuilt + fade * accn_s[b, lines, :]) / total + cen_s[b, h, 1:2, :]
            attended[own_rows, cut] = result.astype(jnp.bfloat16)
    for c in started:
        c.wait_send()


def finish_kernel(length, refresh, attended, w_out, sums, centers, mixed, new_centers, tiles, sem):
    samples, heads, pair, head_dim = new_centers.shape
    count, _, _, tile = tiles.shape
    copies = []
    for n in range(count):
        cut = slice(n * tile, (n + 1) * tile)
        product = jnp.dot(attended[...], w_out[:, cut], preferred_element_type=jnp.float32)
        tiles[n] = product.astype(jnp.bfloat16).reshape(tiles.shape[1:])
        c = pltpu.make_async_copy(tiles.at[n], mixed.at[:, :, pl.ds(n * tile, tile)], sem.at[n])
        c.start()
        copies.append(c)
    for b in range(samples):
        for j in range(pair):
            for h in range(heads):
                line = (b * pair + j) * heads + h
                fresh = sums[line:line + 1, :] / length
                old = centers[b, h, j:j + 1, :]
                new_centers[b, h, j:j + 1, :] = jnp.where(refresh[j, h] == 1, fresh, old)
    for c in copies:
        c.wait()


def per_device(
    seq_count, natural,
    images, w_qkv, b_qkv, q_gain, k_gain, key_basis, value_basis, centers, refresh, w_out
):
    samples, tokens, width = images.shape
    heads, head_dim, rank = key_basis.shape
    key_basis = jnp.swapaxes(key_basis, 1, 2)
    value_basis = jnp.swapaxes(value_basis, 1, 2)
    centers = jnp.transpose(centers, (0, 2, 1, 3))
    side = heads * head_dim
    rows = samples * tokens
    codes = heads * rank
    chips = seq_count // 2
    half = chips // 2
    levels = seq_count.bit_length() - 1
    lines = -(-samples * 2 * heads // 8) * 8
    f32, bf16 = jnp.float32, jnp.bfloat16
    hbm_spec = pl.BlockSpec(memory_space=pltpu.HBM)
    vmem_spec = pl.BlockSpec(memory_space=pltpu.VMEM)
    dma = pltpu.SemaphoreType.DMA
    block = (samples, 2 * codes, tokens)
    stat = pltpu.VMEM((samples, heads * tokens, LANES), f32)
    attended, sums = pl.pallas_call(
        functools.partial(attend_kernel, seq_count, natural),
        out_shape=(
            jax.ShapeDtypeStruct((rows, side), bf16),
            jax.ShapeDtypeStruct((lines, head_dim), f32),
        ),
        in_specs=[hbm_spec] * 8,
        out_specs=(vmem_spec, vmem_spec),
        scratch_shapes=[
            pltpu.VMEM(images.shape, bf16),
            pltpu.VMEM(w_qkv.shape, bf16),
            pltpu.VMEM(b_qkv.shape, f32),
            pltpu.VMEM(q_gain.shape, f32),
            pltpu.VMEM(k_gain.shape, f32),
            pltpu.VMEM(key_basis.shape, f32),
            pltpu.VMEM(value_basis.shape, f32),
            pltpu.VMEM(centers.shape, f32),
            pltpu.VMEM((rows, 2 * side), f32),
            pltpu.VMEM((rows, side), f32),
            pltpu.VMEM((LANES, side), f32),
            pltpu.VMEM((LANES, side), f32),
            pltpu.VMEM((rows, side), f32),
            pltpu.VMEM((rows, side), f32),
            pltpu.VMEM((rows, side), f32),
            pltpu.VMEM((samples, heads * tokens, 2 * LANES), bf16),
            stat, stat, stat, stat, stat,
            pltpu.VMEM(block, bf16),
            pltpu.VMEM((half,) + block, bf16),
            pltpu.VMEM((half,) + block, bf16),
            pltpu.VMEM(block, bf16),
            pltpu.VMEM((half,) + block, bf16),
            pltpu.VMEM((half,) + block, bf16),
            pltpu.VMEM((levels + 1, lines, head_dim), f32),
            pltpu.VMEM((levels, lines, head_dim), f32),
            dma((ROW_CHUNKS + 1,)), dma((ROW_CHUNKS,)), dma((6,)),
            dma((half, samples)), dma((half, samples)), dma((half, samples)), dma((half, samples)),
            dma((samples,)), dma((samples,)),
            dma((half, samples)), dma((half, samples)), dma((half, samples)), dma((half, samples)),
            dma((levels,)), dma((levels,)),
        ],
        compiler_params=pltpu.CompilerParams(
            collective_id=0, has_side_effects=True, vmem_limit_bytes=40 << 20
        ),
        name="attend",
    )(*[
        pltpu.with_memory_space_constraint(a, pltpu.HBM)
        for a in (images, w_qkv, b_qkv, q_gain, k_gain, key_basis, value_basis, centers)
    ])

    tile = width // OUT_TILES
    mixed, new_centers = pl.pallas_call(
        functools.partial(finish_kernel, float(tokens * seq_count)),
        out_shape=(
            jax.ShapeDtypeStruct(images.shape, bf16),
            jax.ShapeDtypeStruct(centers.shape, f32),
        ),
        in_specs=[pl.BlockSpec(memory_space=pltpu.SMEM)] + [vmem_spec] * 4,
        out_specs=(hbm_spec, vmem_spec),
        scratch_shapes=[
            pltpu.VMEM((OUT_TILES, samples, tokens, tile), bf16),
            dma((OUT_TILES,)),
        ],
        compiler_params=pltpu.CompilerParams(vmem_limit_bytes=16 << 20),
        name="finish",
    )(refresh, attended, w_out, sums, centers)
    return mixed, jnp.transpose(new_centers, (0, 2, 1, 3))


def solution(mesh):
    return jax.shard_map(
        functools.partial(per_device, mesh.shape["seq"], natural_ring(mesh)),
        mesh=mesh,
        in_specs=(
            P("groups", "seq", None),
            P(),
            P(),
            P(),
            P(),
            P(),
            P(),
            P("groups", None, None, None),
            P(),
            P(),
        ),
        out_specs=(P("groups", "seq", None), P("groups", None, None, None)),
        check_vma=False,
    )
```
